128 devices in a mesh: section: 4 (over z), dp: 32 (over y, x, core).
Axes of the slice: x: 4, y: 4, z: 4, core: 2. Of those that a mesh axis runs over, the one named last changes fastest.
Arguments:
- hidden: bfloat16 [64, 4, 8192], P('dp')
- delta: float32 [64, 8192], P('dp'), may hold values from -12 to 12
- gain: float32 [8192], replicated, may hold values from 0.5 to 1.5
- head: bfloat16 [131072, 8192], P(('section', 'dp'))
- targets: int32 [64, 3], replicated, may hold values from 0 to 131071
- tlen: int32 [64], replicated, may hold values from 1 to 3, as said below
Outputs:
- edit_loss: float32 [64], P('dp')
- value_step: float32 [64, 8192], P('dp')
The draws below stay inside these ranges and needn't reach their ends.
Inputs may be any that keep to these rules, and one draw needn't show every extreme that they name: Entries of targets at positions tlen or later are not read.
All inputs are finite; a program needn't handle non-finite values.
Results may differ from the reference program's by a relative error of at most 0.0003.
The reference program's roundings to bfloat16 on the way (of `normed`, `base` and `dlogits`) count: a program that leaves them out, or rounds other values in their place, can miss the bound.
Values may be sent and summed in bfloat16 or wider, within the bound.
A program may use at most 128 MiB of HBM per device.

```python
import math
import jax
import jax.numpy as jnp
from jax import lax

D = 8192
TGT = 3
EDITS = 64
VOCAB = 131072


def shared_direction(key):
    return jax.random.normal(jax.random.fold_in(key, 7), (D,), jnp.float32)


def draw_hidden(key, part):
    shape = (EDITS, TGT + 1, D)
    direction = shared_direction(key)
    noise = jax.random.normal(jax.random.fold_in(key, 101), shape, jnp.float32)
    column = jnp.exp(jax.random.uniform(jax.random.fold_in(key, 102), (D,), jnp.float32, 0.0, math.log(10.0)))
    rowscale = jnp.exp(jax.random.uniform(jax.random.fold_in(key, 103), (EDITS, TGT + 1, 1), jnp.float32, 0.0, math.log(10.0)))
    drawn = noise * column * rowscale
    picked = jax.random.randint(jax.random.fold_in(key, 106), (EDITS,), 0, 4) == 0
    picked = picked.at[0].set(True)
    power = jax.random.randint(jax.random.fold_in(key, 107), (EDITS,), 0, 4).astype(jnp.float32)
    amplitude = jnp.exp2(power)[:, None, None]
    small = jax.random.normal(jax.random.fold_in(key, 108), shape, jnp.float32)
    aligned = amplitude * direction[None, None, :] + small
    values = jnp.where(picked[:, None, None], aligned, drawn)
    return values.astype(jnp.bfloat16)


def draw_head(key, part):
    spread = 3.0 / math.sqrt(D)
    weights = jax.random.normal(jax.random.fold_in(key, 201), (VOCAB, D), jnp.float32) * spread
    direction = shared_direction(key)
    anchor = jax.random.randint(jax.random.fold_in(key, 202), (), 0, VOCAB - 1)
    ids = jnp.arange(VOCAB, dtype=jnp.int32)[:, None]
    strength = jnp.where(ids == anchor, 260.0, jnp.where(ids == anchor + 1, 257.5, 0.0))
    weights = weights + strength * direction[None, :] / D
    return weights.astype(jnp.bfloat16)


def draw_tlen(key, part):
    values = jax.random.randint(jax.random.fold_in(key, 301), (EDITS,), 1, TGT + 1)
    values = values.at[0].set(TGT)
    values = values.at[1].set(1)
    return values.astype(jnp.int32)


def plant(entries, stream_key, smallest, high):
    longest = entries.shape.index(max(entries.shape))
    spots = []
    for shift in (0, 1):
        where = [jax.random.randint(jax.random.fold_in(stream_key, axis), (), 0, length) for axis, length in enumerate(entries.shape)]
        where[longest] = (where[longest] + shift) % entries.shape[longest]
        spots.append(tuple(where))
    return entries.at[spots[0]].set(smallest).at[spots[1]].set(high)


def steps_of(own_key, dims, pieces, low, top_value):
    level = 1.0
    for dim, shards_of in pieces:
        heights = jax.random.uniform(jax.random.fold_in(jax.random.fold_in(own_key, 6), dim), (shards_of,), jnp.float32, low / len(pieces), top_value / len(pieces))
        level = level * jnp.repeat(jnp.exp(heights), dims[dim] // shards_of).reshape((-1,) + (1,) * (len(dims) - 1 - dim))
    return level


def centred(rng, shape, scale, limit, split=(), kind=jnp.bfloat16):
    array = scale * jax.random.normal(rng, shape, jnp.float32)
    if split:
        array = array * steps_of(rng, shape, split, -0.22, 0.18)
    return jnp.clip(array, -limit, limit).astype(kind)


def setup_inputs(seed: int = 0) -> dict:
    streams_of = jax.random.split(jax.random.key(seed), 7)
    hidden = draw_hidden(jax.random.fold_in(streams_of[6], 71), 0)
    delta = centred(streams_of[1], (EDITS, D), 2.0, 12.0, ((0, 32),), jnp.float32)
    gain = jnp.clip(1.0 + 0.1 * jax.random.normal(streams_of[2], (D,), jnp.float32), 0.5, 1.5)
    head = draw_head(jax.random.fold_in(streams_of[6], 71), 0)
    targets = plant(jax.random.randint(streams_of[4], (EDITS, TGT), 0, VOCAB), jax.random.fold_in(streams_of[4], 1), 0, VOCAB - 1).astype(jnp.int32)
    tlen = draw_tlen(jax.random.fold_in(streams_of[6], 71), 0)
    return {"hidden": hidden, "delta": delta, "gain": gain, "head": head, "targets": targets, "tlen": tlen}


EPS = 1e-05
KL_WEIGHT = 0.0625
STEP_RATE = 10.0

def normalize(values, gain):
    inv = lax.rsqrt(lax.optimization_barrier(jnp.mean(values * values, axis=-1, keepdims=True)) + EPS)
    return (values * inv * gain, inv)

def reference(hidden, delta, gain, head, targets, tlen):
    hid = hidden.astype(jnp.float32)
    shifted = hid + delta[:, None, :]
    normed, inv = normalize(shifted, gain)
    base, unused = normalize(hid[:, TGT, :], gain)
    rows = jnp.concatenate([normed.astype(jnp.bfloat16), base.astype(jnp.bfloat16)[:, None, :]], axis=1)
    flat = rows.reshape(EDITS * (TGT + 2), D)
    logits = jnp.dot(flat, head.T, preferred_element_type=jnp.float32).reshape(EDITS, TGT + 2, VOCAB)
    top = lax.optimization_barrier(jnp.max(logits, axis=-1, keepdims=True))
    logz = top + jnp.log(lax.optimization_barrier(jnp.sum(jnp.exp(logits - top), axis=-1, keepdims=True)))
    logp = logits - logz
    vocab_ids = jnp.arange(VOCAB, dtype=jnp.int32)
    hit = targets[:, :, None] == vocab_ids[None, None, :]
    tgt_logp = lax.optimization_barrier(jnp.sum(jnp.where(hit, logp[:, :TGT, :], 0.0), axis=-1))
    lengths = tlen.astype(jnp.float32)
    weight = (jnp.arange(TGT, dtype=jnp.int32)[None, :] < tlen[:, None]).astype(jnp.float32) / lengths[:, None]
    nll = -lax.optimization_barrier(jnp.sum(tgt_logp * weight, axis=1))
    base_logp = logp[:, TGT + 1, :]
    base_prob = jnp.exp(base_logp)
    kl = lax.optimization_barrier(jnp.sum(base_prob * (base_logp - logp[:, TGT, :]), axis=-1))
    edit_loss = nll + KL_WEIGHT * kl
    probs = jnp.exp(logp[:, :TGT + 1, :])
    d_target = (probs[:, :TGT, :] - hit.astype(jnp.float32)) * weight[:, :, None]
    d_kl = KL_WEIGHT * (probs[:, TGT, :] - base_prob)
    dlogits = jnp.concatenate([d_target, d_kl[:, None, :]], axis=1).astype(jnp.bfloat16)
    gnorm = jnp.dot(dlogits.reshape(EDITS * (TGT + 1), VOCAB), head, preferred_element_type=jnp.float32).reshape(EDITS, TGT + 1, D)
    scaled = gain * gnorm
    inner = lax.optimization_barrier(jnp.sum(scaled * shifted, axis=-1, keepdims=True))
    gshift = inv * scaled - shifted * inv * inv * inv * inner / D
    value_step = -STEP_RATE * lax.optimization_barrier(jnp.sum(gshift, axis=1))
    return (edit_loss, value_step)
```

```python
import jax
import jax.numpy as jnp
from jax import lax
from jax.sharding import PartitionSpec as P

TGT = 3


EPS = 1e-05
KL_WEIGHT = 0.0625
STEP_RATE = 10.0


def normalize(values, gain):
    inv = lax.rsqrt(jnp.mean(values * values, axis=-1, keepdims=True) + EPS)
    return (values * inv * gain, inv)


def local(hidden, delta, gain, head, targets, tlen):
    edit_dev, slots, width = hidden.shape
    voc_dev = head.shape[0]
    edits = targets.shape[0]
    every = ("section", "dp")
    hid = hidden.astype(jnp.float32)
    shifted = hid + delta[:, None, :]
    normed, inv = normalize(shifted, gain)
    base, unused = normalize(hid[:, slots - 1, :], gain)
    rows = jnp.concatenate(
        [normed.astype(jnp.bfloat16), base.astype(jnp.bfloat16)[:, None, :]], axis=1
    )
    logits = lax.dot_general(
        lax.all_gather(rows, "dp", axis=0, tiled=True),
        head,
        (((2,), (1,)), ((), ())),
        preferred_element_type=jnp.float32,
    )
    local_top = jnp.max(logits, axis=-1)
    local_exp = jnp.exp(logits - local_top[:, :, None])
    local_total = jnp.sum(local_exp, axis=-1)
    gap = jnp.sum(
        local_exp[:, TGT + 1, :] * (logits[:, TGT + 1, :] - logits[:, TGT, :]), axis=-1
    )
    vocab_ids = lax.axis_index(every) * voc_dev + jnp.arange(voc_dev, dtype=jnp.int32)
    hit = targets[:, :, None] == vocab_ids[None, None, :]
    tgt_local = jnp.sum(jnp.where(hit, logits[:, :TGT, :], 0.0), axis=-1)
    packed = jnp.concatenate(
        [
            local_top.reshape(-1),
            local_total.reshape(-1),
            gap,
            tgt_local.reshape(-1),
            inv.reshape(-1),
        ]
    )
    every_stat = lax.all_gather(packed, every)
    n = edits * (TGT + 2)
    tops = every_stat[:, :n].reshape(-1, edits, TGT + 2)
    top = jnp.max(tops, axis=0)
    factor = jnp.exp(tops - top[None])
    total = jnp.sum(every_stat[:, n : 2 * n].reshape(-1, edits, TGT + 2) * factor, axis=0)
    gap_all = jnp.sum(every_stat[:, 2 * n : 2 * n + edits] * factor[:, :, TGT + 1], axis=0)
    first = 2 * n + edits
    tgt_sum = jnp.sum(every_stat[:, first : first + edits * TGT], axis=0).reshape(edits, TGT)
    dp = lax.axis_size("dp")
    inv_all = every_stat[:dp, first + edits * TGT :].reshape(edits, slots)
    logz = top + jnp.log(total)
    kl = gap_all / total[:, TGT + 1] - logz[:, TGT + 1] + logz[:, TGT]
    logp = logits - logz[:, :, None]
    tgt_logp = tgt_sum - logz[:, :TGT]
    lengths = tlen.astype(jnp.float32)
    weight = (jnp.arange(TGT, dtype=jnp.int32)[None, :] < tlen[:, None]).astype(
        jnp.float32
    ) / lengths[:, None]
    nll = -jnp.sum(tgt_logp * weight, axis=1)
    loss_all = nll + KL_WEIGHT * kl
    offset = lax.axis_index("dp") * edit_dev
    edit_loss = lax.dynamic_slice_in_dim(loss_all, offset, edit_dev, 0)
    probs = jnp.exp(logp)
    d_target = (probs[:, :TGT, :] - hit.astype(jnp.float32)) * weight[:, :, None]
    d_kl = KL_WEIGHT * (probs[:, TGT, :] - probs[:, TGT + 1, :])
    dlogits = jnp.concatenate([d_target, d_kl[:, None, :]], axis=1).astype(jnp.bfloat16)
    inner_local = jnp.sum(dlogits.astype(jnp.float32) * logits[:, :slots, :], axis=-1)
    gnorm = jnp.einsum("esv,vd->sed", dlogits, head, preferred_element_type=jnp.float32)
    mixed = jnp.sum(gnorm * inv_all.T[:, :, None], axis=0)
    full, inner = lax.psum((mixed, inner_local), every)
    mine = lax.dynamic_slice_in_dim(full, offset, edit_dev, 0)
    mine_inner = lax.dynamic_slice_in_dim(inner, offset, edit_dev, 0)[:, :, None]
    back = jnp.sum(shifted * (inv * inv * mine_inner / width), axis=1)
    value_step = -STEP_RATE * (gain * mine - back)
    return (edit_loss, value_step)


def solution(mesh):
    placed = (P("dp", None, None), P("dp", None), P(), P(("section", "dp"), None), P(), P())
    return jax.shard_map(
        local, mesh=mesh, in_specs=placed, out_specs=(P("dp"), P("dp", None)), check_vma=False
    )
```

```python
import functools

import jax
import jax.numpy as jnp
from jax import lax
from jax.experimental import pallas as pl
from jax.experimental.pallas import tpu as pltpu
from jax.sharding import PartitionSpec as P

TGT = 3
EPS = 1e-05
KL_WEIGHT = 0.0625
STEP_RATE = 10.0
MESH = pl.DeviceIdType.MESH
F32 = jnp.float32
BF16 = jnp.bfloat16

D = 8192
V = 1024
EDITS = 64
SLICE = 1024
HALF = 512
TILE = 128
UCOLS = TILE + 4 * SLICE


def kernel(
    hidden, delta, gain, head, targets, tlen, step_out, loss_out,
    hv, rows, acc, dl, a2a_src, a2a_in, asm, stc, str_, st1, st2, st3,
    usend, precv, xrecv, zsrc, zrecv, hsem, ssem, rsem,
):
    z = lax.axis_index("section")
    dp = lax.axis_index("dp")
    y = dp // 8
    x = (dp // 2) % 4
    c = dp % 2
    g = dp % 8
    chip = dp // 2
    u = z * 2 + c

    def dev(zz, yy, xx, cc):
        return (zz, (yy * 4 + xx) * 2 + cc)

    def at(v, k):
        return (v + k) % 4

    count = [0]

    def ids(n=1):
        first = count[0]
        count[0] += n
        return first

    def remote(src, dst, i, device):
        return pltpu.make_async_remote_copy(
            src_ref=src, dst_ref=dst, send_sem=ssem.at[i], recv_sem=rsem.at[i],
            device_id=device, device_id_type=MESH,
        )

    sent = []

    def head_copy(k):
        return pltpu.make_async_copy(
            head.at[:, pl.ds(k * SLICE, SLICE)], hv.at[k], hsem.at[k]
        )

    for k in range(8):
        head_copy(k).start()

    barrier = pltpu.get_barrier_semaphore()
    peers = []
    for j in range(1, 16):
        peers.append(dev(z, at(y, j // 4), at(x, j % 4), c))
    for j in range(4):
        peers.append(dev(z, y, at(x, j), 1 - c))
    for j in range(1, 4):
        peers.append(dev(at(z, j), y, x, c))
        peers.append(dev(at(z, j), y, x, 1 - c))
    for p in peers:
        pl.semaphore_signal(barrier, inc=1, device_id=p, device_id_type=MESH)

    dlt = delta[...]
    gn = gain[...]
    invs = []
    for s in range(5):
        val = hidden[:, min(s, 3), :].astype(F32)
        if s < 4:
            val = val + dlt
        inv = lax.rsqrt(jnp.mean(val * val, axis=-1, keepdims=True) + EPS)
        invs.append(inv)
        out = (val * inv * gn).astype(BF16)
        for k in range(8):
            a2a_src[k, s] = out[:, k * SLICE : (k + 1) * SLICE]

    pl.semaphore_wait(barrier, len(peers))

    base = ids(8)
    a2a = []
    for j in range(1, 8):
        to = (g + j) % 8
        cp = remote(a2a_src.at[to], a2a_in.at[g], base + j, (z, y * 8 + to))
        cp.start()
        a2a.append(cp)
    sent += a2a
    a2a_in[g] = a2a_src[g]
    for cp in a2a:
        cp.wait_recv()
    for s in range(5):
        for k in range(8):
            asm[s, 2 * k : 2 * k + 2, :] = a2a_in[k, s].astype(F32)
    for s in range(5):
        piece = asm[s].astype(BF16)
        rows[c, x, 0, s, y] = piece[:, :HALF]
        rows[c, x, 1, s, y] = piece[:, HALF:]

    LO, HI = pl.ds(0, 256), pl.ds(256, 256)
    XP, XM = dev(z, y, at(x, 1), c), dev(z, y, at(x, 3), c)
    YP, YM = dev(z, at(y, 1), x, c), dev(z, at(y, 3), x, c)
    PART = dev(z, y, x, 1 - c)

    class Ring:
        KEYS = ("+lo", "-hi", "+hi", "-lo", "f+", "f-")

        def __init__(self, block, plus, minus, place):
            self.block, self.plus, self.minus, self.place = block, plus, minus, place
            self.first = ids(6)

        def copy(self, key):
            where = {"f+": 3, "f-": 1}.get(key, 0)
            q = LO if key in ("+lo", "-lo", "f+") else HI
            device = self.plus if key in ("+lo", "+hi", "f+") else self.minus
            ref = self.block(at(self.place, where), q)
            return remote(ref, ref, self.first + self.KEYS.index(key), device)

        def start(self):
            for key in self.KEYS[:4]:
                self.copy(key).start()

        def relay(self):
            self.copy("+lo").wait_recv()
            self.copy("f+").start()
            self.copy("-hi").wait_recv()
            self.copy("f-").start()

        def near(self, which):
            self.copy(which).wait_recv()

        def far(self):
            self.copy("f+").wait_recv()
            self.copy("f-").wait_recv()

        def drain(self):
            for key in self.KEYS:
                self.copy(key).wait_send()

    a1 = Ring(lambda w, q: rows.at[c, x, 0, :, w, :, q], YP, YM, y)
    b1 = Ring(lambda w, q: rows.at[c, w, 1, :, y, :, q], XP, XM, x)
    a2 = Ring(lambda w, q: rows.at[c, w, 0, :, :, :, q], XP, XM, x)
    b2 = {
        k: Ring(lambda w, q, k=k: rows.at[c, at(x, k), 1, :, w, :, q], YP, YM, y)
        for k in range(4)
    }
    pair_ids = ids(8)

    def pair(k, h):
        ref = rows.at[c, at(x, k), h]
        return remote(ref, ref, pair_ids + 2 * k + h, PART)

    def give(k, h):
        pair(k, h).start()

    def take(k, h):
        pair(k, h).wait_recv()

    acc[...] = jnp.zeros_like(acc)
    a1.start()
    b1.start()
    b2[0].start()
    a1.relay()
    b1.relay()
    a1.near("+hi")
    a1.near("-lo")
    a1.far()
    a2.start()
    give(0, 0)
    b1.near("+hi")
    b2[3].start()
    b1.near("-lo")
    b2[1].start()
    for k in range(8):
        head_copy(k).wait()

    def s1():
        b1.far()
        b2[2].start()
        b2[0].relay()
        take(0, 0)

    def s2():
        b2[0].near("+hi")
        b2[0].near("-lo")
        a2.relay()
        b2[0].far()
        give(0, 1)

    def s3():
        b2[3].relay()
        take(0, 1)

    def s4():
        a2.near("+hi")
        give(3, 0)

    def s5():
        a2.near("-lo")
        give(1, 0)
        b2[1].relay()

    def s6():
        take(3, 0)

    def s7():
        take(1, 0)

    def s8():
        b2[2].relay()
        b2[3].near("+hi")
        b2[3].near("-lo")
        b2[3].far()
        give(3, 1)

    def s9():
        b2[1].near("+hi")
        b2[1].near("-lo")
        b2[1].far()
        give(1, 1)

    def s10():
        take(3, 1)

    def s11():
        take(1, 1)

    def s12():
        a2.far()
        give(2, 0)

    def s13():
        b2[2].near("+hi")
        b2[2].near("-lo")
        b2[2].far()
        give(2, 1)

    def s14():
        take(2, 0)

    def s15():
        take(2, 1)

    actions = [None, s1, s2, s3, s4, s5, s6, s7, s8, s9, s10, s11, s12, s13, s14, s15]
    order = [
        (0, 0, 0), (1, 0, 0), (0, 0, 1), (1, 0, 1),
        (0, 3, 0), (0, 1, 0), (1, 3, 0), (1, 1, 0),
        (0, 3, 1), (0, 1, 1), (1, 3, 1), (1, 1, 1),
        (0, 2, 0), (0, 2, 1), (1, 2, 0), (1, 2, 1),
    ]

    def pick(t, values):
        out = t * 0 + values[0]
        for k, v in enumerate(values):
            if k:
                out = jnp.where(t == k, v, out)
        return out

    def step(t, carry):
        for k, act in enumerate(actions):
            if act is not None:
                pl.when(t == k)(act)
        rc = pick(t, [o[0] for o in order])
        rx = pick(t, [o[1] for o in order])
        h = pick(t, [o[2] for o in order])
        cc = (c + rc) % 2
        xx = (x + rx) % 4
        lhs = rows[cc, xx, h].reshape(5 * EDITS, HALF)
        rhs = hv[xx * 2 + cc, :, pl.ds(pl.multiple_of(h * HALF, HALF), HALF)]
        acc[...] += lax.dot_general(
            lhs, rhs, (((1,), (1,)), ((), ())), preferred_element_type=F32
        )
        return carry

    lax.fori_loop(0, 16, step, 0)

    lane = lax.broadcasted_iota(jnp.int32, (EDITS, TILE), 1)
    row = lax.broadcasted_iota(jnp.int32, (EDITS, 1), 0)
    first = (z * 32 + dp) * V
    vocab = first + lax.broadcasted_iota(jnp.int32, (1, V), 1)

    def logits(s):
        return acc[s * EDITS : (s + 1) * EDITS, :]

    stc[5 * EDITS :, :] = jnp.zeros((EDITS, TILE), F32)
    for s in range(5):
        lg = logits(s)
        top = jnp.max(lg, axis=-1, keepdims=True)
        ex = jnp.exp(lg - top)
        tot = jnp.sum(ex, axis=-1, keepdims=True)
        if s < TGT:
            hit = targets[:, s : s + 1] == vocab
            extra = jnp.sum(jnp.where(hit, lg, 0.0), axis=-1, keepdims=True)
        elif s == TGT:
            extra = jnp.zeros((EDITS, 1), F32)
        else:
            extra = jnp.sum(ex * (lg - logits(TGT)), axis=-1, keepdims=True)
        put = jnp.where(lane == 0, top, jnp.where(lane == 1, tot, extra))
        if s < 4:
            iv = invs[s]
            ivc = jnp.where(
                row == 2 * dp, iv[0:1, :], jnp.where(row == 2 * dp + 1, iv[1:2, :], 0.0)
            )
            put = jnp.where(lane == 3, ivc, put)
        stc[s * EDITS : (s + 1) * EDITS, :] = put

    lane3 = lax.broadcasted_iota(jnp.int32, (1, 3 * TILE), 1)
    row8 = lax.broadcasted_iota(jnp.int32, (8, 3 * TILE), 0)

    def combine(ref, n):
        vals = [ref[k] for k in range(n)]
        top = vals[0][0:1]
        keep = vals[0][3:4]
        for v in vals[1:]:
            top = jnp.maximum(top, v[0:1])
            keep = jnp.maximum(keep, v[3:4])
        tot = jnp.zeros_like(top)
        extra = jnp.zeros_like(top)
        for v in vals:
            f = jnp.exp(v[0:1] - top)
            tot = tot + v[1:2] * f
            extra = extra + v[2:3] * jnp.where(lane3 >= 4 * EDITS, f, 1.0)
        return top, tot, extra, keep

    def pack(a, b, d, e):
        return jnp.where(
            row8 == 0, a, jnp.where(row8 == 1, b, jnp.where(row8 == 2, d, e))
        )

    def exchange(ref, me, n, device):
        first_id = ids(n)
        cps = []
        for j in range(1, n):
            cp = remote(ref.at[me], ref.at[me], first_id + j, device(j))
            cp.start()
            cps.append(cp)
        for cp in cps:
            cp.wait_recv()
        sent.extend(cps)

    st1[g] = stc[...].T[0:8, :]
    exchange(st1, g, 8, lambda j: (z, y * 8 + (g + j) % 8))
    st2[y] = pack(*combine(st1, 8))
    exchange(st2, y, 4, lambda j: dev(z, at(y, j), x, c))
    st3[z] = pack(*combine(st2, 4))
    exchange(st3, z, 4, lambda j: dev(at(z, j), y, x, c))
    top, tot, extra, keep = combine(st3, 4)
    extra = jnp.where(lane3 >= 4 * EDITS, extra / tot, extra)
    str_[0:8, :] = pack(top + jnp.log(tot), extra, keep, keep)
    str_[8:, :] = jnp.zeros((TILE - 8, 3 * TILE), F32)
    stc[...] = str_[...].T

    def col(s, k):
        return stc[s * EDITS : (s + 1) * EDITS, k : k + 1]

    lens = tlen[...]
    inner = jnp.zeros((EDITS, TILE), F32)
    loss = KL_WEIGHT * (col(4, 1) - col(4, 0) + col(3, 0))
    for s in range(4):
        lg = logits(s)
        prob = jnp.exp(lg - col(s, 0))
        if s < TGT:
            hit = (targets[:, s : s + 1] == vocab).astype(F32)
            wt = (s < lens).astype(F32) / lens.astype(F32)
            dg = (prob - hit) * wt
            loss = loss - jnp.where(s < lens, (col(s, 1) - col(s, 0)) * wt, 0.0)
        else:
            dg = KL_WEIGHT * (prob - jnp.exp(logits(4) - col(4, 0)))
        dg = dg.astype(BF16)
        dl[s * EDITS : (s + 1) * EDITS, :] = dg
        part = jnp.sum(dg.astype(F32) * lg, axis=-1, keepdims=True)
        inner = jnp.where(lane == s, part, inner)
    for i in range(2):
        own = jnp.where(row == 2 * dp + i, loss, 0.0)
        loss_out[i : i + 1, :] = jnp.broadcast_to(
            jnp.sum(own, axis=0, keepdims=True), (1, TILE)
        )

    for k in range(16):
        usend[0, k, :, 0:TILE] = inner[4 * k : 4 * k + 4, :]
        usend[1, k, :, 0:TILE] = jnp.zeros((4, TILE), F32)

    p_ids = ids(5)
    x_ids = ids(16 * 5)
    z_ids = ids(8 * 5)

    def cols_of(n):
        return pl.ds(pl.multiple_of(TILE + n * SLICE, TILE), SLICE)

    COL0 = pl.ds(0, TILE)

    def give_half(n, cols):
        return remote(usend.at[1 - c, :, :, cols], precv.at[:, :, cols], p_ids + n, PART)

    def x_copy(n, cols, j):
        yy, xx = at(y, j // 4), at(x, j % 4)
        return remote(
            usend.at[c, yy * 4 + xx, :, cols], xrecv.at[chip, :, cols],
            x_ids + n * 16 + j, dev(z, yy, xx, c),
        )

    def z_copy(n, cols, j):
        to = (u + j) % 8
        return remote(
            zsrc.at[to % 2, :, cols], zrecv.at[u, :, cols],
            z_ids + n * 8 + j, dev(to // 2, y, x, to % 2),
        )

    def loop(lo, hi, body):
        def run(j, carry):
            body(j)
            return carry
        lax.fori_loop(lo, hi, run, 0)

    def spread(n, cols):
        give_half(n, cols).wait_recv()
        both = usend[c, :, :, cols] + precv[:, :, cols]
        usend[c, :, :, cols] = both
        xrecv[chip, :, cols] = usend[c, chip, :, cols]
        loop(1, 16, lambda j: x_copy(n, cols, j).start())

    def plane(n, cols):
        loop(1, 16, lambda j: x_copy(n, cols, j).wait_recv())
        total = xrecv[0, :, cols]
        for k in range(1, 16):
            total = total + xrecv[k, :, cols]
        for k in range(2):
            zsrc[k, :, cols] = total[2 * k : 2 * k + 2, :]
        zrecv[u, :, cols] = zsrc[c, :, cols]
        loop(1, 8, lambda j: z_copy(n, cols, j).start())

    def part(n, sub):
        grad = jnp.dot(dl[...], hv[2 * n + sub], preferred_element_type=F32)
        mix = grad[0:EDITS] * col(0, 2)
        for s in range(1, 4):
            mix = mix + grad[s * EDITS : (s + 1) * EDITS] * col(s, 2)
        for k in range(16):
            usend[sub, k, :, cols_of(n)] = mix[4 * k : 4 * k + 4, :]

    give_half(4, COL0).start()

    def grads(n):
        part(n, 1 - c)
        give_half(n, cols_of(n)).start()
        pl.when(n == 0)(lambda: spread(4, COL0))
        pl.when(n > 0)(lambda: spread(n - 1, cols_of(n - 1)))
        part(n, c)

    loop(0, 4, grads)
    spread(3, cols_of(3))
    plane(4, COL0)
    loop(0, 4, lambda n: plane(n, cols_of(n)))

    loop(1, 8, lambda j: z_copy(4, COL0, j).wait_recv())
    inn = zrecv[0, :, 0:TILE]
    for k in range(1, 8):
        inn = inn + zrecv[k, :, 0:TILE]
    coef = [invs[s] * invs[s] * inn[:, s : s + 1] / D for s in range(4)]
    for n in range(4):
        loop(1, 8, lambda j: z_copy(n, cols_of(n), j).wait_recv())
        for hf in range(2):
            cols = pl.ds((2 * n + hf) * SLICE, SLICE)
            mine = zrecv[hf, :, cols_of(n)]
            for k in range(1, 4):
                mine = mine + zrecv[2 * k + hf, :, cols_of(n)]
            shift = delta[:, cols]
            back = jnp.zeros((2, SLICE), F32)
            for s in range(4):
                back = back + (hidden[:, s, cols].astype(F32) + shift) * coef[s]
            step_out[:, cols] = -STEP_RATE * (gain[:, cols] * mine - back)

    for cp in sent:
        cp.wait_send()
    for ring in [a1, b1, a2] + [b2[k] for k in range(4)]:
        ring.drain()
    for k in range(4):
        for h in range(2):
            pair(k, h).wait_send()
    give_half(4, COL0).wait_send()
    loop(1, 16, lambda j: x_copy(4, COL0, j).wait_send())
    loop(1, 8, lambda j: z_copy(4, COL0, j).wait_send())

    def drain(n):
        give_half(n, cols_of(n)).wait_send()
        loop(1, 16, lambda j: x_copy(n, cols_of(n), j).wait_send())
        loop(1, 8, lambda j: z_copy(n, cols_of(n), j).wait_send())

    loop(0, 4, drain)
    assert count[0] <= SEMS


SEMS = 256


def local(hidden, delta, gain, head, targets, tlen):
    vm = pl.BlockSpec(memory_space=pltpu.VMEM)
    scratch = [
        pltpu.VMEM((8, V, SLICE), BF16),
        pltpu.VMEM((2, 4, 2, 5, 4, 16, HALF), BF16),
        pltpu.VMEM((5 * EDITS, V), F32),
        pltpu.VMEM((4 * EDITS, V), BF16),
        pltpu.VMEM((8, 5, 2, SLICE), BF16),
        pltpu.VMEM((8, 5, 2, SLICE), BF16),
        pltpu.VMEM((5, 16, SLICE), F32),
        pltpu.VMEM((3 * TILE, TILE), F32),
        pltpu.VMEM((TILE, 3 * TILE), F32),
        pltpu.VMEM((8, 8, 3 * TILE), F32),
        pltpu.VMEM((4, 8, 3 * TILE), F32),
        pltpu.VMEM((4, 8, 3 * TILE), F32),
        pltpu.VMEM((2, 16, 4, UCOLS), F32),
        pltpu.VMEM((16, 4, UCOLS), F32),
        pltpu.VMEM((16, 4, UCOLS), F32),
        pltpu.VMEM((2, 2, UCOLS), F32),
        pltpu.VMEM((8, 2, UCOLS), F32),
        pltpu.SemaphoreType.DMA((8,)),
        pltpu.SemaphoreType.DMA((SEMS,)),
        pltpu.SemaphoreType.DMA((SEMS,)),
    ]
    step, loss = pl.pallas_call(
        kernel,
        out_shape=(
            jax.ShapeDtypeStruct((2, D), F32),
            jax.ShapeDtypeStruct((2, TILE), F32),
        ),
        in_specs=[vm, vm, vm, pl.BlockSpec(memory_space=pl.ANY), vm, vm],
        out_specs=(vm, vm),
        scratch_shapes=scratch,
        compiler_params=pltpu.CompilerParams(
            collective_id=0, has_side_effects=True, vmem_limit_bytes=56 * 2**20
        ),
    )(hidden, delta, gain.reshape(1, D), head, targets, tlen.reshape(EDITS, 1))
    return (loss[:, 0], step)


def solution(mesh):
    placed = (P("dp", None, None), P("dp", None), P(), P(("section", "dp"), None), P(), P())
    return jax.shard_map(
        local, mesh=mesh, in_specs=placed, out_specs=(P("dp"), P("dp", None)), check_vma=False
    )
```
